32 devices in a mesh: row: 2 (over x), col: 16 (over z, y, core).
Axes of the slice: x: 2, y: 2, z: 4, core: 2. Of those that a mesh axis runs over, the one named last changes fastest.
Arguments:
- tile_values: float32 [2, 16, 64, 128, 128], P('row', 'col'), may hold values from -0.21875 to 0.21875
- tile_rows: int32 [2, 16, 64], P('row', 'col'), may hold values from 0 to 159, as said below
- tile_cols: int32 [2, 16, 64], P('row', 'col'), may hold values from 0 to 23
- x_start: float32 [384, 128], P('col', 'row'), may hold values from -6 to 6
- z_start: float32 [320, 128], P('row'), may hold values from -6 to 6
- y_start: float32 [320, 128], P('row'), may hold values from -3 to 3
- lower_bound: float32 [320, 128], P('row'), may hold values from -1.5 to -0.1
- upper_bound: float32 [320, 128], P('row'), may hold values from 0.1 to 1.5
- cost_diag: float32 [384, 128], P('col', 'row'), may hold values from 0.1 to 10
- linear: float32 [384, 128], P('col', 'row'), may hold values from -6 to 6
- penalty: float32 [1], replicated, may hold values from 0.3 to 3
- proximal: float32 [1], replicated, may hold values from 0.1 to 1
- relaxation: float32 [1], replicated, may hold values from 1.2 to 1.8
Outputs:
- x_next: float32 [384, 128], P('col', 'row')
- z_next: float32 [320, 128], P('row')
- y_next: float32 [320, 128], P('row')
The draws below stay inside these ranges and needn't reach their ends.
Inputs may be any that keep to these rules, and one draw needn't show every extreme that they name: On each device the 64 pairs (tile_rows, tile_cols) are distinct.
All inputs are finite; a program needn't handle non-finite values.
Results may differ from the reference program's by a relative error of at most 0.0002.
Values sent between devices are 32-bit elements; how exact they have to be, the bound alone decides.
No kernel may reach another device: no remote copies, remote signals or barrier semaphores. Data moves between devices by JAX's collectives and lax.ppermute only.
A program may use at most 64 MiB of HBM per device.

```python
import math
import jax
import jax.numpy as jnp
from jax import lax

BS = 128
XB = 24
ZB = 160
TPD = 64
ADMM_ITERS = 2
CG_STEPS = 1
NB = 384
MB = 320
N_ROW = 2
N_COL = 16


def tile_pattern(key):
    folded = jax.random.fold_in(key, 7)
    subkeys = jax.random.split(folded, N_ROW * N_COL)
    chosen = jax.vmap(lambda subkey: jax.random.permutation(subkey, ZB * XB)[:TPD])(subkeys)
    chosen = chosen.reshape(N_ROW, N_COL, TPD).astype(jnp.int32)
    return (chosen // XB, chosen % XB)


def draw_tile_rows(key, part):
    return tile_pattern(key)[0]


def draw_tile_cols(key, part):
    return tile_pattern(key)[1]


def steps_of(rng, extent, cuts, smallest, high):
    def one(dim, shards_of):
        heights = jax.random.uniform(jax.random.fold_in(jax.random.fold_in(rng, 6), dim), (shards_of,), jnp.float32, smallest / len(cuts), high / len(cuts))
        return jnp.repeat(jnp.exp(heights), extent[dim] // shards_of).reshape((-1,) + (1,) * (len(extent) - dim - 1))

    factor_of = one(*cuts[0])
    for cut in cuts[1:]:
        factor_of = factor_of * one(*cut)
    return factor_of


def scatter_about(own_key, shape, width, most, cuts=(), kind=jnp.bfloat16):
    drawn = jax.random.normal(own_key, shape, jnp.float32) * width
    if len(cuts) > 0:
        drawn = steps_of(own_key, shape, cuts, -0.22, 0.18) * drawn
    return jnp.clip(drawn, min=-most, max=most).astype(kind)


def setup_inputs(seed: int = 0) -> dict:
    keys = jax.random.split(jax.random.key(seed), 14)
    tile_values = scatter_about(keys[0], (N_ROW, N_COL, TPD, BS, BS), (BS * TPD * N_COL // ZB) ** -0.5, 0.21875, ((0, 2), (1, 16)), jnp.float32)
    tile_rows = draw_tile_rows(jax.random.fold_in(keys[13], 71), 0)
    tile_cols = draw_tile_cols(jax.random.fold_in(keys[13], 71), 0)
    x_start = scatter_about(keys[3], (NB, BS), 1.0, 6.0, ((0, 16), (1, 2)), jnp.float32)
    z_start = scatter_about(keys[4], (MB, BS), 1.0, 6.0, ((0, 2),), jnp.float32)
    y_start = scatter_about(keys[5], (MB, BS), 0.5, 3.0, ((0, 2),), jnp.float32)
    lower_bound = jnp.clip(-1.5 + 1.4 * jax.random.uniform(keys[6], (MB, BS), jnp.float32) ** steps_of(keys[6], (MB, BS), ((0, 2),), -0.2, 0.2), -1.5, -0.1)
    upper_bound = jnp.clip(0.1 + 1.4 * jax.random.uniform(keys[7], (MB, BS), jnp.float32) ** steps_of(keys[7], (MB, BS), ((0, 2),), -0.2, 0.2), 0.1, 1.5)
    cost_diag = jnp.clip(jnp.exp(math.log(10.0) - 4.6051702 * jax.random.uniform(keys[8], (NB, BS), jnp.float32) ** steps_of(keys[8], (NB, BS), ((0, 16), (1, 2)), -0.2, 0.2)), 0.1, 10.0)
    linear = scatter_about(keys[9], (NB, BS), 1.0, 6.0, ((0, 16), (1, 2)), jnp.float32)
    penalty = jnp.clip(jnp.exp(jax.random.uniform(keys[10], (1,), jnp.float32, math.log(0.3), math.log(3.0))), 0.3, 3.0)
    proximal = jnp.clip(jnp.exp(jax.random.uniform(keys[11], (1,), jnp.float32, math.log(0.1), math.log(1.0))), 0.1, 1.0)
    relaxation = jnp.clip(jax.random.uniform(keys[12], (1,), jnp.float32, 1.2, 1.8), 1.2, 1.8)
    return {"tile_values": tile_values, "tile_rows": tile_rows, "tile_cols": tile_cols, "x_start": x_start, "z_start": z_start, "y_start": y_start, "lower_bound": lower_bound, "upper_bound": upper_bound, "cost_diag": cost_diag, "linear": linear, "penalty": penalty, "proximal": proximal, "relaxation": relaxation}


HIGH = lax.Precision.HIGHEST


def block_indices(tile_rows, tile_cols):
    row_base = jnp.arange(N_ROW, dtype=jnp.int32)[:, None, None] * ZB
    col_base = jnp.arange(N_COL, dtype=jnp.int32)[None, :, None] * XB
    return (tile_rows + row_base).reshape(-1), (tile_cols + col_base).reshape(-1)


def forward_apply(flat_tiles, global_rows, global_cols, vector):
    picked = jnp.take(vector, global_cols, axis=0)
    products = jnp.einsum("kij,kj->ki", flat_tiles, picked, precision=HIGH)
    return jax.ops.segment_sum(products, global_rows, num_segments=MB)


def backward_apply(flat_tiles, global_rows, global_cols, weights_rows):
    picked = jnp.take(weights_rows, global_rows, axis=0)
    products = jnp.einsum("kij,ki->kj", flat_tiles, picked, precision=HIGH)
    return jax.ops.segment_sum(products, global_cols, num_segments=NB)


def reference(tile_values, tile_rows, tile_cols, x_start, z_start, y_start, lower_bound, upper_bound, cost_diag, linear, penalty, proximal, relaxation):
    flat_tiles = tile_values.reshape(-1, BS, BS)
    global_rows, global_cols = block_indices(tile_rows, tile_cols)
    rho_value = penalty[0]
    sigma_value = proximal[0]
    relax_value = relaxation[0]
    x_now, z_now, y_now = x_start, z_start, y_start
    for outer_round in range(ADMM_ITERS):
        image_now = forward_apply(flat_tiles, global_rows, global_cols, x_now)
        target = rho_value * z_now - y_now - rho_value * image_now
        residual = -linear - cost_diag * x_now + backward_apply(flat_tiles, global_rows, global_cols, target)
        guess = x_now
        direction = residual
        norm_now = jnp.sum(residual * residual)
        for inner_round in range(CG_STEPS):
            pushed = forward_apply(flat_tiles, global_rows, global_cols, direction)
            applied = (cost_diag + sigma_value) * direction + rho_value * backward_apply(flat_tiles, global_rows, global_cols, pushed)
            step_length = norm_now / jnp.sum(direction * applied)
            guess = guess + step_length * direction
            residual = residual - step_length * applied
            norm_next = jnp.sum(residual * residual)
            direction = residual + (norm_next / norm_now) * direction
            norm_now = norm_next
        z_tilde = forward_apply(flat_tiles, global_rows, global_cols, guess)
        x_now = relax_value * guess + (1.0 - relax_value) * x_now
        mixed = relax_value * z_tilde + (1.0 - relax_value) * z_now
        z_fresh = jnp.minimum(jnp.maximum(mixed + y_now / rho_value, lower_bound), upper_bound)
        y_now = y_now + rho_value * (mixed - z_fresh)
        z_now = z_fresh
    return x_now, z_now, y_now
```

```python
import jax
import jax.numpy as jnp
from jax import lax
from jax.sharding import PartitionSpec as P

ADMM_ITERS = 2


HIGH = lax.Precision.HIGHEST


def butterfly(value, axis, size):
    if size & (size - 1):
        return lax.psum(value, axis)
    step = 1
    while step < size:
        value = value + lax.ppermute(value, axis, [(i, i ^ step) for i in range(size)])
        step *= 2
    return value


def shards(
    n_row,
    n_col,
    tile_values,
    tile_rows,
    tile_cols,
    x_start,
    z_start,
    y_start,
    lower_bound,
    upper_bound,
    cost_diag,
    linear,
    penalty,
    proximal,
    relaxation,
):
    order_size = tile_values.shape[3]
    flat_tiles = tile_values.reshape(-1, order_size, order_size)
    row_index = tile_rows.reshape(-1)
    col_index = tile_cols.reshape(-1)
    count_tiles = row_index.shape[0]
    block_rows = z_start.shape[0]
    block_cols, part = x_start.shape
    row_table = (
        lax.broadcasted_iota(jnp.int32, (block_rows, count_tiles), 0) == row_index[None, :]
    ).astype(jnp.float32)
    col_table = (
        lax.broadcasted_iota(jnp.int32, (block_cols, count_tiles), 0) == col_index[None, :]
    ).astype(jnp.float32)
    rho = penalty[0]
    sigma = proximal[0]
    alpha = relaxation[0]

    def forward(vector):
        picked = jnp.take(vector, col_index, axis=0)
        products = jnp.einsum("kij,kj->ki", flat_tiles, picked, precision=HIGH)
        return jnp.dot(row_table, products, precision=HIGH)

    def backward(weights_rows):
        picked = jnp.take(weights_rows, row_index, axis=0)
        products = jnp.einsum("kij,ki->kj", flat_tiles, picked, precision=HIGH)
        return jnp.dot(col_table, products, precision=HIGH)

    packed = jnp.concatenate([x_start, cost_diag, linear], axis=0)
    packed = lax.all_gather(packed, "row", axis=1, tiled=True)
    x_now, diag, line = jnp.split(packed, 3, axis=0)
    z_now, y_now = z_start, y_start
    image = butterfly(forward(x_now), "col", n_col)
    for _ in range(ADMM_ITERS):
        target = rho * z_now - y_now - rho * image
        residual = butterfly(backward(target), "row", n_row) - line - diag * x_now
        rr = jnp.sum(residual * residual)
        rdr = jnp.sum((diag + sigma) * residual * residual)
        extra = jnp.concatenate(
            [jnp.full((1, order_size), rr), jnp.full((1, order_size), rdr), jnp.zeros((6, order_size), jnp.float32)]
        )
        pushed = butterfly(jnp.concatenate([forward(residual), extra]), "col", n_col)
        norm, bent = pushed[block_rows, 0], pushed[block_rows + 1, 0]
        pushed = pushed[:block_rows]
        spread = butterfly(jnp.full((8, order_size), jnp.sum(pushed * pushed)), "row", n_row)[0, 0]
        step = norm / (bent + rho * spread)
        mixed = alpha * (image + step * pushed) + (1.0 - alpha) * z_now
        image = image + (alpha * step) * pushed
        x_now = x_now + (alpha * step) * residual
        z_fresh = jnp.minimum(jnp.maximum(mixed + y_now / rho, lower_bound), upper_bound)
        y_now = y_now + rho * (mixed - z_fresh)
        z_now = z_fresh
    mine = lax.dynamic_slice_in_dim(x_now, lax.axis_index("row") * part, part, 1)
    return mine, z_now, y_now


def solution(mesh):
    placed = (
        P("row", "col", None, None, None),
        P("row", "col", None),
        P("row", "col", None),
        P("col", "row"),
        P("row", None),
        P("row", None),
        P("row", None),
        P("row", None),
        P("col", "row"),
        P("col", "row"),
        P(),
        P(),
        P(),
    )
    n_row, n_col = mesh.shape["row"], mesh.shape["col"]
    return jax.shard_map(
        lambda *args: shards(n_row, n_col, *args),
        mesh=mesh,
        in_specs=placed,
        out_specs=(P("col", "row"), P("row", None), P("row", None)),
        check_vma=False,
    )
```

```python
import functools

import jax
import jax.numpy as jnp
from jax import lax
from jax.experimental import pallas as pl
from jax.experimental.pallas import tpu as pltpu
from jax.sharding import PartitionSpec as P

ADMM_ITERS = 2
SUB = 8
F32 = jnp.float32
BF16 = jnp.bfloat16


VMEM = pl.BlockSpec(memory_space=pltpu.VMEM)
SMEM = pl.BlockSpec(memory_space=pltpu.SMEM)


def split2(value):
    high = value.astype(BF16).astype(F32)
    return high, (value - high).astype(BF16).astype(F32)


def split3(value):
    high = value.astype(BF16)
    rest = value - high.astype(F32)
    mid = rest.astype(BF16)
    return high, mid, (rest - mid.astype(F32)).astype(BF16)


def place(piece, slot, width):
    blocks, part = piece.shape
    if part == width:
        return piece
    full = jnp.concatenate([piece, jnp.zeros((blocks, width - part), F32)], axis=1)
    return pltpu.roll(full, slot * part, 1)


def lane_total(row):
    return jnp.sum(row, axis=1, keepdims=True)


def write_windows(win, value):
    blocks = value.shape[0]
    high, low = split2(value)
    win[pl.ds(0, blocks, stride=2), :] = high
    win[pl.ds(1, blocks, stride=2), :] = low
    win[pl.ds(2 * blocks, SUB), :] = jnp.zeros((SUB, value.shape[1]), F32)


def scatter(table, prod):
    parts = jnp.concatenate(split3(prod[...]), axis=0)
    return lax.dot_general(table[...], parts, (((1,), (0,)), ((), ())), preferred_element_type=F32)


def forward_product(win, tiles, index, prod):
    for k in range(prod.shape[0]):
        window = win[pl.ds(2 * index[k], SUB), :].astype(BF16)
        both = jnp.concatenate([window, window], axis=1)
        out = lax.dot_general(both, tiles[k], (((1,), (1,)), ((), ())), preferred_element_type=F32)
        prod[k : k + 1, :] = out[0:1] + out[1:2]


def backward_product(win, tiles, index, prod):
    size = prod.shape[1]
    for k in range(prod.shape[0]):
        window = win[pl.ds(2 * index[k], SUB), :].astype(BF16)
        out = lax.dot_general(window, tiles[k], (((1,), (0,)), ((), ())), preferred_element_type=F32)
        out = out[0:2, :size] + out[0:2, size:]
        prod[k : k + 1, :] = out[0:1] + out[1:2]


def prepare_kernel(blocks_z, blocks_x, tiles, rows, cols, rho, sigma, alpha, x, d, q, packed, row_table, col_table, scalars, x_at, d_at, q_at):
    size = tiles.shape[2]
    value = tiles[...]
    high = value.astype(BF16)
    packed[:, :, :size] = high
    packed[:, :, size:] = (value - high.astype(F32)).astype(BF16)

    @pl.when(pl.program_id(0) == 0)
    def _():
        count = rows.shape[1]
        half = blocks_z // 2
        core = lax.rem(lax.axis_index("col"), 2)
        spot = lax.broadcasted_iota(jnp.int32, (blocks_z, count), 0) + core * half
        spot = jnp.where(spot >= blocks_z, spot - blocks_z, spot)
        hit = jnp.where(spot == rows[...], 1.0, 0.0)
        row_table[...] = jnp.concatenate([hit, hit, hit], axis=1).astype(BF16)
        hit = jnp.where(lax.broadcasted_iota(jnp.int32, (blocks_x, count), 0) == cols[...], 1.0, 0.0)
        col_table[...] = jnp.concatenate([hit, hit, hit], axis=1).astype(BF16)
        for i, ref in enumerate((rho, sigma, alpha)):
            scalars[i : i + 1, :] = jnp.full((1, size), ref[0], F32)
        scalars[3:SUB, :] = jnp.zeros((SUB - 3, size), F32)
        slot = lax.axis_index("row")
        for ref, out in ((x, x_at), (d, d_at), (q, q_at)):
            out[...] = place(ref[...], slot, size)


def first_kernel(others, cols, x_at, *refs):
    pieces, (tiles, row_table, mine, other, win, prod) = refs[:others], refs[others:]
    size = x_at.shape[1]
    n_row = others + 1
    full = x_at[...]
    for k in range(others):
        full = full + place(pieces[k][...], lax.rem(lax.axis_index("row") + n_row - 1 - k, n_row), size)
    write_windows(win, full)
    forward_product(win, tiles, cols, prod)
    out = scatter(row_table, prod)
    half = mine.shape[0]
    mine[...] = out[:half]
    other[...] = out[half:]


def forward_kernel(cols, own, received, d_at, scalars, slots, tiles, row_table, mine, other, residual, win, prod):
    r = own[...] + received[...]
    residual[...] = r
    write_windows(win, r)
    forward_product(win, tiles, cols, prod)
    out = scatter(row_table, prod)
    half = out.shape[0] // 2
    mine[:half] = out[:half]
    other[:half] = out[half:]
    size = r.shape[1]
    part = size // slots
    lane = lax.broadcasted_iota(jnp.int32, (1, size), 1)
    slot = lax.axis_index("row")
    here = jnp.where((lane >= slot * part) & (lane < (slot + 1) * part), 1.0, 0.0)
    bent = (d_at[...] + scalars[1:2, :] * here) * r * r
    extra = jnp.concatenate(
        [jnp.sum(r * r, axis=0, keepdims=True), jnp.sum(bent, axis=0, keepdims=True), jnp.zeros((SUB - 2, size), F32)],
        axis=0,
    )
    mine[half:] = extra
    other[half:] = extra


def join(target, mine, other):
    half = target.shape[0] // 2
    core = lax.rem(lax.axis_index("col"), 2)
    target[pl.ds(pl.multiple_of(core * half, SUB), half), :] = mine[:half]
    target[pl.ds(pl.multiple_of((1 - core) * half, SUB), half), :] = other[:half]


def back_kernel(rows, mine, other, z, y, x_at, d_at, q_at, scalars, tiles, col_table, partial, image, win, prod):
    join(image, mine, other)
    rho = scalars[0:1, :]
    write_windows(win, rho * z[...] - y[...] - rho * image[...])
    backward_product(win, tiles, rows, prod)
    partial[...] = scatter(col_table, prod) - q_at[...] - d_at[...] * x_at[...]


def step_of(norms, spread, rho):
    return lane_total(norms[0:1]) / (lane_total(spread[1:2]) + rho * lane_total(spread[0:1]))


def update(pushed, image, z, y, low, up, step, rho, alpha):
    mixed = alpha * (image + step * pushed) + (1.0 - alpha) * z
    z_new = jnp.minimum(jnp.maximum(mixed + y / rho, low), up)
    return z_new, y + rho * (mixed - z_new)


def middle_kernel(rows, mine, other, norms, spread, image, z, y, low, up, x_at, residual, d_at, q_at, scalars, slots, tiles, col_table, partial, image_new, z_new, y_new, x_new, win, prod):
    join(image_new, mine, other)
    rho, alpha = scalars[0:1, :], scalars[2:3, :]
    step = step_of(norms[...], spread[...], rho[:, 0:1])
    pushed = image_new[...]
    z_next, y_next = update(pushed, image[...], z[...], y[...], low[...], up[...], step, rho, alpha)
    fresh = image[...] + (alpha * step) * pushed
    image_new[...] = fresh
    z_new[...] = z_next
    y_new[...] = y_next
    write_windows(win, rho * z_next - y_next - rho * fresh)
    backward_product(win, tiles, rows, prod)
    size = x_at.shape[1]
    part = size // slots
    lane = lax.broadcasted_iota(jnp.int32, (1, size), 1)
    slot = lax.axis_index("row")
    here = jnp.where((lane >= slot * part) & (lane < (slot + 1) * part), 1.0, 0.0)
    x = x_at[...] + (alpha * step * here) * residual[...]
    x_new[...] = x
    partial[...] = scatter(col_table, prod) - q_at[...] - d_at[...] * x


def last_kernel(mine, other, norms, spread, image, z, y, low, up, x_at, residual, scalars, slots, x_out, z_out, y_out, pushed):
    join(pushed, mine, other)
    rho, alpha = scalars[0:1, :], scalars[2:3, :]
    step = step_of(norms[...], spread[...], rho[:, 0:1])
    z_next, y_next = update(pushed[...], image[...], z[...], y[...], low[...], up[...], step, rho, alpha)
    z_out[...] = z_next
    y_out[...] = y_next
    x = x_at[...] + (alpha * step) * residual[...]
    size = x_at.shape[1]
    part = size // slots
    if slots > 1:
        x = pltpu.roll(x, lax.rem(slots - lax.axis_index("row"), slots) * part, 1)
    x_out[...] = x[:, :part]


def flip(size, step):
    return [(i, i ^ step) for i in range(size)]


def butterfly(value, axis, size, first=1):
    step = first
    while step < size:
        value = value + lax.ppermute(value, axis, flip(size, step))
        step *= 2
    return value


def shards(n_row, n_col, tile_values, tile_rows, tile_cols, x, z, y, low, up, d, q, penalty, proximal, relaxation):
    count, size = tile_values.shape[2], tile_values.shape[3]
    tiles = tile_values.reshape(count, size, size)
    rows, cols = tile_rows.reshape(1, count), tile_cols.reshape(1, count)
    rows_s, cols_s = tile_rows.reshape(count), tile_cols.reshape(count)
    bz, (bx, part) = z.shape[0], x.shape
    half = bz // 2
    big = jax.ShapeDtypeStruct((bz, size), F32)
    small = jax.ShapeDtypeStruct((bx, size), F32)

    def call(kernel, name, out_shape, scratch=(), n_smem=0, grid_spec=None):
        def run(*args):
            return pl.pallas_call(
                kernel,
                out_shape=out_shape,
                in_specs=[SMEM] * n_smem + [VMEM] * (len(args) - n_smem),
                out_specs=jax.tree.map(lambda _: VMEM, out_shape),
                scratch_shapes=list(scratch),
                name=name,
            )(*args)

        return run

    def wins(blocks):
        return [pltpu.VMEM((2 * blocks + SUB, size), F32), pltpu.VMEM((count, size), F32)]

    pieces = [lax.ppermute(x, "row", [(i, (i + s) % n_row) for i in range(n_row)]) for s in range(1, n_row)]

    chunk = 8 if count % 8 == 0 else count
    whole = lambda shape: pl.BlockSpec(shape, lambda i: (0,) * len(shape))
    packed, row_table, col_table, scalars, x_at, d_at, q_at = pl.pallas_call(
        functools.partial(prepare_kernel, bz, bx),
        grid=(count // chunk,),
        in_specs=[pl.BlockSpec((chunk, size, size), lambda i: (i, 0, 0)), whole((1, count)), whole((1, count)), SMEM, SMEM, SMEM]
        + [whole((bx, part))] * 3,
        out_specs=[pl.BlockSpec((chunk, size, 2 * size), lambda i: (i, 0, 0)), whole((bz, 3 * count)), whole((bx, 3 * count)), whole((SUB, size))]
        + [whole((bx, size))] * 3,
        out_shape=[
            jax.ShapeDtypeStruct((count, size, 2 * size), BF16),
            jax.ShapeDtypeStruct((bz, 3 * count), BF16),
            jax.ShapeDtypeStruct((bx, 3 * count), BF16),
            jax.ShapeDtypeStruct((SUB, size), F32),
            small,
            small,
            small,
        ],
        name="prepare",
    )(tiles, rows, cols, penalty, proximal, relaxation, x, d, q)

    def reduce_half(mine, other):
        mine = mine + lax.ppermute(other, "col", flip(n_col, 1))
        return butterfly(mine, "col", n_col, 2)

    def swap(mine):
        return lax.ppermute(mine, "col", flip(n_col, 1))

    halves = [jax.ShapeDtypeStruct((half, size), F32)] * 2
    mine, other = call(functools.partial(first_kernel, n_row - 1), "first", halves, wins(bx), 1)(
        cols_s, x_at, *pieces, packed, row_table
    )
    mine = reduce_half(mine, other)
    partial, image = call(back_kernel, "back", [small, big], wins(bz), 1)(
        rows_s, mine, swap(mine), z, y, x_at, d_at, q_at, scalars, packed, col_table
    )
    tall = [jax.ShapeDtypeStruct((half + SUB, size), F32)] * 2
    for turn in range(ADMM_ITERS):
        own = butterfly(partial, "row", n_row // 2) if n_row > 1 else partial
        received = lax.ppermute(own, "row", flip(n_row, n_row // 2)) if n_row > 1 else jnp.zeros_like(own)

        def forward_body(a, b, c, e, f, *rest):
            forward_kernel(a, b, c, e, f, n_row, *rest)

        mine, other, residual = call(forward_body, "forward", tall + [small], wins(bx), 1)(
            cols_s, own, received, d_at, scalars, packed, row_table
        )
        mine = reduce_half(mine, other)
        other = swap(mine)
        squares = jnp.sum(mine[:half] ** 2, axis=0, keepdims=True) + jnp.sum(other[:half] ** 2, axis=0, keepdims=True)
        spread = jnp.concatenate([squares, mine[half + 1 :]], axis=0)
        spread = butterfly(spread, "row", n_row)
        norms = mine[half:]
        if turn + 1 < ADMM_ITERS:

            def middle_body(*refs):
                middle_kernel(*refs[:15], n_row, *refs[15:])

            partial, image, z, y, x_at = call(middle_body, "middle", [small, big, big, big, small], wins(bz), 1)(
                rows_s, mine, other, norms, spread, image, z, y, low, up, x_at, residual, d_at, q_at, scalars, packed, col_table
            )
        else:

            def last_body(*refs):
                last_kernel(*refs[:12], n_row, *refs[12:])

            shapes = [jax.ShapeDtypeStruct((bx, part), F32), big, big]
            return tuple(
                call(last_body, "last", shapes, [pltpu.VMEM((bz, size), F32)])(
                    mine, other, norms, spread, image, z, y, low, up, x_at, residual, scalars
                )
            )


def solution(mesh):
    placed = (
        P("row", "col", None, None, None),
        P("row", "col", None),
        P("row", "col", None),
        P("col", "row"),
        P("row", None),
        P("row", None),
        P("row", None),
        P("row", None),
        P("col", "row"),
        P("col", "row"),
        P(),
        P(),
        P(),
    )
    n_row, n_col = mesh.shape["row"], mesh.shape["col"]
    return jax.shard_map(
        lambda *args: shards(n_row, n_col, *args),
        mesh=mesh,
        in_specs=placed,
        out_specs=(P("col", "row"), P("row", None), P("row", None)),
        check_vma=False,
    )
```

```python
import functools

import jax
import jax.numpy as jnp
from jax import lax
from jax.experimental import pallas as pl
from jax.experimental.pallas import tpu as pltpu
from jax.sharding import PartitionSpec as P

ADMM_ITERS = 2
SUB = 8
F32 = jnp.float32
BF16 = jnp.bfloat16
LIMIT = 24 << 20


VMEM = pl.BlockSpec(memory_space=pltpu.VMEM)
SMEM = pl.BlockSpec(memory_space=pltpu.SMEM)


def split2(value):
    high = value.astype(BF16).astype(F32)
    return high, (value - high).astype(BF16).astype(F32)


def split3(value):
    high = value.astype(BF16)
    rest = value - high.astype(F32)
    mid = rest.astype(BF16)
    return high, mid, (rest - mid.astype(F32)).astype(BF16)


def place(piece, slot, width):
    blocks, part = piece.shape
    if part == width:
        return piece
    full = jnp.concatenate([piece, jnp.zeros((blocks, width - part), F32)], axis=1)
    return pltpu.roll(full, slot * part, 1)


def lane_total(row):
    return jnp.sum(row, axis=1, keepdims=True)


def write_windows(win, value):
    blocks = value.shape[0]
    high, low = split2(value)
    win[pl.ds(0, blocks, stride=2), :] = high
    win[pl.ds(1, blocks, stride=2), :] = low
    win[pl.ds(2 * blocks, SUB), :] = jnp.zeros((SUB, value.shape[1]), F32)


def scatter(table, prod):
    parts = jnp.concatenate(split3(prod[...]), axis=0)
    return lax.dot_general(table[...], parts, (((1,), (0,)), ((), ())), preferred_element_type=F32)


def forward_product(win, tiles, index, prod):
    for k in range(prod.shape[0]):
        window = win[pl.ds(2 * index[k], SUB), :].astype(BF16)
        both = jnp.concatenate([window, window], axis=1)
        out = lax.dot_general(both, tiles[k], (((1,), (1,)), ((), ())), preferred_element_type=F32)
        prod[k : k + 1, :] = out[0:1] + out[1:2]


def backward_product(win, tiles, index, prod):
    size = prod.shape[1]
    for k in range(prod.shape[0]):
        window = win[pl.ds(2 * index[k], SUB), :].astype(BF16)
        out = lax.dot_general(window, tiles[k], (((1,), (0,)), ((), ())), preferred_element_type=F32)
        out = out[0:2, :size] + out[0:2, size:]
        prod[k : k + 1, :] = out[0:1] + out[1:2]


def prepare_kernel(blocks_z, blocks_x, tiles, rows, cols, x, d, q, packed, row_table, col_table, x_at, d_at, q_at, held, rows_v, cols_v, x_v, d_v, q_v, sems):
    size = tiles.shape[2]
    count = tiles.shape[0]
    small = [(rows, rows_v), (cols, cols_v), (x, x_v), (d, d_v), (q, q_v)]
    chunks = sems.shape[0] - len(small)
    chunk = count // chunks
    fetches = [pltpu.make_async_copy(ref, out, sems.at[chunks + i]) for i, (ref, out) in enumerate(small)]
    copies = [
        pltpu.make_async_copy(tiles.at[pl.ds(i * chunk, chunk)], held.at[pl.ds(i * chunk, chunk)], sems.at[i])
        for i in range(chunks)
    ]
    for copy in fetches + copies:
        copy.start()
    for copy in fetches:
        copy.wait()
    half = blocks_z // 2
    core = lax.rem(lax.axis_index("col"), 2)
    spot = lax.broadcasted_iota(jnp.int32, (blocks_z, count), 0) + core * half
    spot = jnp.where(spot >= blocks_z, spot - blocks_z, spot)
    hit = jnp.where(spot == rows_v[...], 1.0, 0.0)
    row_table[...] = jnp.concatenate([hit, hit, hit], axis=1).astype(BF16)
    hit = jnp.where(lax.broadcasted_iota(jnp.int32, (blocks_x, count), 0) == cols_v[...], 1.0, 0.0)
    col_table[...] = jnp.concatenate([hit, hit, hit], axis=1).astype(BF16)
    slot = lax.axis_index("row")
    for ref, out in ((x_v, x_at), (d_v, d_at), (q_v, q_at)):
        out[...] = place(ref[...], slot, size)
    for i, copy in enumerate(copies):
        copy.wait()
        for k in range(i * chunk, (i + 1) * chunk):
            value = held[k]
            high = value.astype(BF16)
            packed[k, :, :size] = high
            packed[k, :, size:] = (value - high.astype(F32)).astype(BF16)


def first_kernel(others, cols, x_at, *refs):
    pieces, (tiles, row_table, mine, other, win, prod) = refs[:others], refs[others:]
    size = x_at.shape[1]
    n_row = others + 1
    full = x_at[...]
    for k in range(others):
        full = full + place(pieces[k][...], lax.rem(lax.axis_index("row") + n_row - 1 - k, n_row), size)
    write_windows(win, full)
    forward_product(win, tiles, cols, prod)
    out = scatter(row_table, prod)
    half = mine.shape[0]
    mine[...] = out[:half]
    other[...] = out[half:]


def forward_kernel(cols, own, received, d_at, scalars, slots, tiles, row_table, mine, other, residual, win, prod):
    r = own[...] + received[...]
    residual[...] = r
    write_windows(win, r)
    forward_product(win, tiles, cols, prod)
    out = scatter(row_table, prod)
    half = out.shape[0] // 2
    mine[:half] = out[:half]
    other[:half] = out[half:]
    size = r.shape[1]
    part = size // slots
    lane = lax.broadcasted_iota(jnp.int32, (1, size), 1)
    slot = lax.axis_index("row")
    here = jnp.where((lane >= slot * part) & (lane < (slot + 1) * part), 1.0, 0.0)
    bent = (d_at[...] + scalars[1:2, :] * here) * r * r
    extra = jnp.concatenate(
        [jnp.sum(r * r, axis=0, keepdims=True), jnp.sum(bent, axis=0, keepdims=True), jnp.zeros((SUB - 2, size), F32)],
        axis=0,
    )
    mine[half:] = extra
    other[half:] = extra


def join(target, mine, other):
    half = target.shape[0] // 2
    core = lax.rem(lax.axis_index("col"), 2)
    target[pl.ds(pl.multiple_of(core * half, SUB), half), :] = mine[:half]
    target[pl.ds(pl.multiple_of((1 - core) * half, SUB), half), :] = other[:half]


def back_kernel(rows, mine, other, z, y, x_at, d_at, q_at, scalars, tiles, col_table, partial, image, win, prod):
    join(image, mine, other)
    rho = scalars[0:1, :]
    write_windows(win, rho * z[...] - y[...] - rho * image[...])
    backward_product(win, tiles, rows, prod)
    partial[...] = scatter(col_table, prod) - q_at[...] - d_at[...] * x_at[...]


def step_of(mine, other, rho):
    half = mine.shape[0] - SUB
    spread = mine[half + 1 : half + 2] + other[half + 1 : half + 2]
    return lane_total(mine[half : half + 1]) / (lane_total(mine[half + 2 : half + 3]) + rho * lane_total(spread))


def update(pushed, image, z, y, low, up, step, rho, alpha):
    mixed = alpha * (image + step * pushed) + (1.0 - alpha) * z
    z_new = jnp.minimum(jnp.maximum(mixed + y / rho, low), up)
    return z_new, y + rho * (mixed - z_new)


def middle_kernel(rows, mine, other, image, z, y, low, up, x_at, residual, d_at, q_at, scalars, slots, tiles, col_table, partial, image_new, z_new, y_new, x_new, win, prod):
    join(image_new, mine, other)
    rho, alpha = scalars[0:1, :], scalars[2:3, :]
    step = step_of(mine, other, rho[:, 0:1])
    pushed = image_new[...]
    z_next, y_next = update(pushed, image[...], z[...], y[...], low[...], up[...], step, rho, alpha)
    fresh = image[...] + (alpha * step) * pushed
    image_new[...] = fresh
    z_new[...] = z_next
    y_new[...] = y_next
    write_windows(win, rho * z_next - y_next - rho * fresh)
    backward_product(win, tiles, rows, prod)
    size = x_at.shape[1]
    part = size // slots
    lane = lax.broadcasted_iota(jnp.int32, (1, size), 1)
    slot = lax.axis_index("row")
    here = jnp.where((lane >= slot * part) & (lane < (slot + 1) * part), 1.0, 0.0)
    x = x_at[...] + (alpha * step * here) * residual[...]
    x_new[...] = x
    partial[...] = scatter(col_table, prod) - q_at[...] - d_at[...] * x


def last_kernel(mine, other, image, z, y, low, up, x_at, residual, scalars, slots, x_out, z_out, y_out, pushed):
    join(pushed, mine, other)
    rho, alpha = scalars[0:1, :], scalars[2:3, :]
    step = step_of(mine, other, rho[:, 0:1])
    z_next, y_next = update(pushed[...], image[...], z[...], y[...], low[...], up[...], step, rho, alpha)
    z_out[...] = z_next
    y_out[...] = y_next
    x = x_at[...] + (alpha * step) * residual[...]
    size = x_at.shape[1]
    part = size // slots
    if slots > 1:
        x = pltpu.roll(x, lax.rem(slots - lax.axis_index("row"), slots) * part, 1)
    x_out[...] = x[:, :part]


def flip(size, step):
    return [(i, i ^ step) for i in range(size)]


def butterfly(value, axis, size, first=1):
    step = first
    while step < size:
        value = value + lax.ppermute(value, axis, flip(size, step))
        step *= 2
    return value


def shards(n_row, n_col, tile_values, tile_rows, tile_cols, x, z, y, low, up, d, q, penalty, proximal, relaxation):
    count, size = tile_values.shape[2], tile_values.shape[3]
    tiles = tile_values.reshape(count, size, size)
    rows, cols = tile_rows.reshape(1, count), tile_cols.reshape(1, count)
    rows_s, cols_s = tile_rows.reshape(count), tile_cols.reshape(count)
    bz, (bx, part) = z.shape[0], x.shape
    half = bz // 2
    big = pltpu.VMEM((bz, size), F32)
    small = pltpu.VMEM((bx, size), F32)
    out_big = jax.ShapeDtypeStruct((bz, size), F32)

    def call(kernel, name, out_shape, scratch=(), n_smem=0, grid_spec=None):
        def run(*args):
            args = [
                pltpu.with_memory_space_constraint(a, pltpu.SMEM if i < n_smem else pltpu.VMEM)
                for i, a in enumerate(args)
            ]
            return pl.pallas_call(
                kernel,
                out_shape=out_shape,
                in_specs=[SMEM] * n_smem + [VMEM] * (len(args) - n_smem),
                out_specs=[VMEM] * len(out_shape),
                scratch_shapes=list(scratch),
                compiler_params=pltpu.CompilerParams(vmem_limit_bytes=LIMIT),
                name=name,
            )(*args)

        return run

    def wins(blocks):
        return [pltpu.VMEM((2 * blocks + SUB, size), F32), pltpu.VMEM((count, size), F32)]

    pieces = [lax.ppermute(x, "row", [(i, (i + s) % n_row) for i in range(n_row)]) for s in range(1, n_row)]

    chunks = 8 if count % 8 == 0 else 1
    given = [pltpu.with_memory_space_constraint(a, pltpu.HBM) for a in (tiles, rows, cols, x, d, q)]
    packed, row_table, col_table, x_at, d_at, q_at = pl.pallas_call(
        functools.partial(prepare_kernel, bz, bx),
        in_specs=[pl.BlockSpec(memory_space=pltpu.HBM)] * 6,
        out_specs=[VMEM] * 6,
        out_shape=[
            pltpu.VMEM((count, size, 2 * size), BF16),
            pltpu.VMEM((bz, 3 * count), BF16),
            pltpu.VMEM((bx, 3 * count), BF16),
            small,
            small,
            small,
        ],
        scratch_shapes=[pltpu.VMEM((count, size, size), F32)]
        + [pltpu.VMEM((1, count), jnp.int32)] * 2
        + [pltpu.VMEM((bx, part), F32)] * 3
        + [pltpu.SemaphoreType.DMA((chunks + 5,))],
        compiler_params=pltpu.CompilerParams(vmem_limit_bytes=LIMIT),
        name="prepare",
    )(*given)
    scalars = jnp.stack([penalty[0], proximal[0], relaxation[0]])
    scalars = jnp.broadcast_to(jnp.pad(scalars, (0, SUB - 3))[:, None], (SUB, size))

    bits = [1 << i for i in range(1, n_col.bit_length() - 1)]

    def by_bits(value, some):
        some = list(some)
        while some:
            if len(some) == 1:
                return value + lax.ppermute(value, "col", flip(n_col, some[0]))
            one, two = some[0], some[1]
            both = lax.ppermute(value, "col", flip(n_col, one | two))
            first = lax.ppermute(value, "col", flip(n_col, one))
            second = lax.ppermute(value, "col", flip(n_col, two))
            value = (value + first) + (second + both)
            some = some[2:]
        return value

    def core_sum(mine, other):
        return mine + lax.ppermute(other, "col", flip(n_col, 1))

    def reduce_half(mine, other):
        return by_bits(core_sum(mine, other), bits)

    def reduce_pushed(mine, other):
        value = core_sum(mine, other)
        if n_row == 2 and bits:
            value = by_bits(value, bits[:-1])
            across = lambda mask: lax.ppermute(value, ("row", "col"), flip(n_row * n_col, mask))
            far = across(n_col | bits[-1])
            here, beside = across(bits[-1]), across(n_col)
            value = value + here
            away = beside + far
            squares = jnp.sum(value[:half] ** 2, axis=0, keepdims=True) + jnp.sum(away[:half] ** 2, axis=0, keepdims=True)
            bent = value[half + 1 : half + 2] + away[half + 1 : half + 2]
        else:
            value = by_bits(value, bits)
            squares = jnp.sum(value[:half] ** 2, axis=0, keepdims=True)
            sums = butterfly(jnp.concatenate([squares, value[half + 1 :]], axis=0), "row", n_row)
            squares, bent = sums[0:1], sums[1:2]
        below = [value[half : half + 1], squares, bent, value[half + 3 :]]
        mine = jnp.concatenate([value[:half]] + below, axis=0)
        return mine, swap(mine)

    def swap(mine):
        return lax.ppermute(mine, "col", flip(n_col, 1))

    halves = [pltpu.VMEM((half, size), F32)] * 2
    mine, other = call(functools.partial(first_kernel, n_row - 1), "first", halves, wins(bx), 1)(
        cols_s, x_at, *pieces, packed, row_table
    )
    mine = reduce_half(mine, other)
    partial, image = call(back_kernel, "back", [small, big], wins(bz), 1)(
        rows_s, mine, swap(mine), z, y, x_at, d_at, q_at, scalars, packed, col_table
    )
    tall = [pltpu.VMEM((half + SUB, size), F32)] * 2
    for turn in range(ADMM_ITERS):
        own = butterfly(partial, "row", n_row // 2) if n_row > 1 else partial
        received = lax.ppermute(own, "row", flip(n_row, n_row // 2)) if n_row > 1 else jnp.zeros_like(own)

        def forward_body(a, b, c, e, f, *rest):
            forward_kernel(a, b, c, e, f, n_row, *rest)

        mine, other, residual = call(forward_body, "forward", tall + [small], wins(bx), 1)(
            cols_s, own, received, d_at, scalars, packed, row_table
        )
        mine, other = reduce_pushed(mine, other)
        if turn + 1 < ADMM_ITERS:

            def middle_body(*refs):
                middle_kernel(*refs[:13], n_row, *refs[13:])

            partial, image, z, y, x_at = call(middle_body, "middle", [small, big, big, big, small], wins(bz), 1)(
                rows_s, mine, other, image, z, y, low, up, x_at, residual, d_at, q_at, scalars, packed, col_table
            )
        else:

            def last_body(*refs):
                last_kernel(*refs[:10], n_row, *refs[10:])

            shapes = [jax.ShapeDtypeStruct((bx, part), F32), out_big, out_big]
            return tuple(
                call(last_body, "last", shapes, [pltpu.VMEM((bz, size), F32)])(
                    mine, other, image, z, y, low, up, x_at, residual, scalars
                )
            )


def solution(mesh):
    placed = (
        P("row", "col", None, None, None),
        P("row", "col", None),
        P("row", "col", None),
        P("col", "row"),
        P("row", None),
        P("row", None),
        P("row", None),
        P("row", None),
        P("col", "row"),
        P("col", "row"),
        P(),
        P(),
        P(),
    )
    n_row, n_col = mesh.shape["row"], mesh.shape["col"]
    return jax.shard_map(
        lambda *args: shards(n_row, n_col, *args),
        mesh=mesh,
        in_specs=placed,
        out_specs=(P("col", "row"), P("row", None), P("row", None)),
        check_vma=False,
    )
```

```python
import functools

import jax
import jax.numpy as jnp
from jax import lax
from jax.experimental import pallas as pl
from jax.experimental.pallas import tpu as pltpu
from jax.sharding import PartitionSpec as P

ADMM_ITERS = 2
SUB = 8
F32 = jnp.float32
BF16 = jnp.bfloat16
LIMIT = 24 << 20


VMEM = pl.BlockSpec(memory_space=pltpu.VMEM)


def split2(value):
    high = value.astype(BF16).astype(F32)
    return high, (value - high).astype(BF16).astype(F32)


def split3(value):
    high = value.astype(BF16)
    rest = value - high.astype(F32)
    mid = rest.astype(BF16)
    return high, mid, (rest - mid.astype(F32)).astype(BF16)


def place(piece, slot, width):
    blocks, part = piece.shape
    if part == width:
        return piece
    full = jnp.concatenate([piece, jnp.zeros((blocks, width - part), F32)], axis=1)
    return pltpu.roll(full, slot * part, 1)


def lane_total(row):
    return jnp.sum(row, axis=1, keepdims=True)


def pick(table, value):
    parts = jnp.concatenate(split2(value), axis=1).astype(BF16)
    return lax.dot_general(table[...], parts, (((1,), (0,)), ((), ())), preferred_element_type=F32)


def scatter(table, prod):
    parts = jnp.concatenate(split3(prod), axis=0)
    return lax.dot_general(table[...], parts, (((1,), (0,)), ((), ())), preferred_element_type=F32)


def product(picked, tiles):
    count, size = tiles.shape[0], tiles.shape[1]
    row = lax.broadcasted_iota(jnp.int32, (SUB, size), 0)
    blocks = []
    for m in range(0, count, SUB):
        left = jnp.concatenate([picked[m : m + SUB, :size], picked[m : m + SUB, size:]], axis=0).astype(BF16)
        block = jnp.zeros((SUB, size), F32)
        for k in range(SUB):
            out = lax.dot_general(left, tiles[m + k], (((1,), (0,)), ((), ())), preferred_element_type=F32)
            out = out[:SUB] + out[SUB:]
            block = jnp.where(row == k, out[:, :size] + out[:, size:], block)
        blocks.append(block)
    return jnp.concatenate(blocks, axis=0)


def upright(row):
    count = row.shape[1]
    shape = (count, count)
    here = lax.broadcasted_iota(jnp.int32, shape, 0) == lax.broadcasted_iota(jnp.int32, shape, 1)
    return jnp.sum(jnp.where(here, row.astype(F32), 0.0), axis=1, keepdims=True)


def named(column, blocks):
    lane = lax.broadcasted_iota(jnp.int32, (column.shape[0], blocks), 1).astype(F32)
    return jnp.where(lane == column, 1.0, 0.0).astype(BF16)


def prepare_kernel(blocks_z, blocks_x, tiles, rows, cols, x, d, q, packed, turned, row_table, col_table, row_pick, col_pick, x_at, d_at, q_at, held, rows_v, cols_v, x_v, d_v, q_v, sems):
    size = tiles.shape[2]
    count = tiles.shape[0]
    small = [(rows, rows_v), (cols, cols_v), (x, x_v), (d, d_v), (q, q_v)]
    chunks = sems.shape[0] - len(small)
    chunk = count // chunks
    fetches = [pltpu.make_async_copy(ref, out, sems.at[chunks + i]) for i, (ref, out) in enumerate(small)]
    copies = [
        pltpu.make_async_copy(tiles.at[pl.ds(i * chunk, chunk)], held.at[pl.ds(i * chunk, chunk)], sems.at[i])
        for i in range(chunks)
    ]
    for copy in fetches + copies:
        copy.start()
    for copy in fetches:
        copy.wait()
    half = blocks_z // 2
    core = lax.rem(lax.axis_index("col"), 2)
    spot = lax.broadcasted_iota(jnp.int32, (blocks_z, count), 0) + core * half
    spot = jnp.where(spot >= blocks_z, spot - blocks_z, spot)
    hit = jnp.where(spot == rows_v[...], 1.0, 0.0)
    row_table[...] = jnp.concatenate([hit, hit, hit], axis=1).astype(BF16)
    hit = jnp.where(lax.broadcasted_iota(jnp.int32, (blocks_x, count), 0) == cols_v[...], 1.0, 0.0)
    col_table[...] = jnp.concatenate([hit, hit, hit], axis=1).astype(BF16)
    row_pick[...] = named(upright(rows_v[...]), blocks_z)
    col_pick[...] = named(upright(cols_v[...]), blocks_x)
    slot = lax.axis_index("row")
    for ref, out in ((x_v, x_at), (d_v, d_at), (q_v, q_at)):
        out[...] = place(ref[...], slot, size)
    for i, copy in enumerate(copies):
        copy.wait()
        for k in range(i * chunk, (i + 1) * chunk):
            value = held[k]
            high = value.astype(BF16)
            low = (value - high.astype(F32)).astype(BF16)
            packed[k, :, :size] = high
            packed[k, :, size:] = low
            turned[k, :, :size] = high.T
            turned[k, :, size:] = low.T


def first_kernel(others, x_at, *refs):
    pieces, (tiles, pick_table, row_table, mine, other) = refs[:others], refs[others:]
    size = x_at.shape[1]
    n_row = others + 1
    full = x_at[...]
    for k in range(others):
        full = full + place(pieces[k][...], lax.rem(lax.axis_index("row") + n_row - 1 - k, n_row), size)
    out = scatter(row_table, product(pick(pick_table, full), tiles))
    half = mine.shape[0]
    mine[...] = out[:half]
    other[...] = out[half:]


def forward_kernel(own, received, d_at, scalars, slots, tiles, pick_table, row_table, mine, other, residual):
    r = own[...] + received[...]
    residual[...] = r
    out = scatter(row_table, product(pick(pick_table, r), tiles))
    half = out.shape[0] // 2
    mine[:half] = out[:half]
    other[:half] = out[half:]
    size = r.shape[1]
    part = size // slots
    lane = lax.broadcasted_iota(jnp.int32, (1, size), 1)
    slot = lax.axis_index("row")
    here = jnp.where((lane >= slot * part) & (lane < (slot + 1) * part), 1.0, 0.0)
    bent = (d_at[...] + scalars[1:2, :] * here) * r * r
    extra = jnp.concatenate(
        [jnp.sum(r * r, axis=0, keepdims=True), jnp.sum(bent, axis=0, keepdims=True), jnp.zeros((SUB - 2, size), F32)],
        axis=0,
    )
    mine[half:] = extra
    other[half:] = extra


def join(target, mine, other):
    half = target.shape[0] // 2
    core = lax.rem(lax.axis_index("col"), 2)
    target[pl.ds(pl.multiple_of(core * half, SUB), half), :] = mine[:half]
    target[pl.ds(pl.multiple_of((1 - core) * half, SUB), half), :] = other[:half]


def back_kernel(mine, other, z, y, x_at, d_at, q_at, scalars, tiles, pick_table, col_table, partial, image):
    join(image, mine, other)
    rho = scalars[0:1, :]
    target = rho * z[...] - y[...] - rho * image[...]
    out = scatter(col_table, product(pick(pick_table, target), tiles))
    partial[...] = out - q_at[...] - d_at[...] * x_at[...]


def step_of(mine, other, rho):
    half = mine.shape[0] - SUB
    spread = mine[half + 1 : half + 2] + other[half + 1 : half + 2]
    return lane_total(mine[half : half + 1]) / (lane_total(mine[half + 2 : half + 3]) + rho * lane_total(spread))


def update(pushed, image, z, y, low, up, step, rho, alpha):
    mixed = alpha * (image + step * pushed) + (1.0 - alpha) * z
    z_new = jnp.minimum(jnp.maximum(mixed + y / rho, low), up)
    return z_new, y + rho * (mixed - z_new)


def middle_kernel(mine, other, image, z, y, low, up, x_at, residual, d_at, q_at, scalars, slots, tiles, pick_table, col_table, partial, image_new, z_new, y_new, x_new):
    join(image_new, mine, other)
    rho, alpha = scalars[0:1, :], scalars[2:3, :]
    step = step_of(mine, other, rho[:, 0:1])
    pushed = image_new[...]
    z_next, y_next = update(pushed, image[...], z[...], y[...], low[...], up[...], step, rho, alpha)
    fresh = image[...] + (alpha * step) * pushed
    image_new[...] = fresh
    z_new[...] = z_next
    y_new[...] = y_next
    out = scatter(col_table, product(pick(pick_table, rho * z_next - y_next - rho * fresh), tiles))
    size = x_at.shape[1]
    part = size // slots
    lane = lax.broadcasted_iota(jnp.int32, (1, size), 1)
    slot = lax.axis_index("row")
    here = jnp.where((lane >= slot * part) & (lane < (slot + 1) * part), 1.0, 0.0)
    x = x_at[...] + (alpha * step * here) * residual[...]
    x_new[...] = x
    partial[...] = out - q_at[...] - d_at[...] * x


def last_kernel(mine, other, image, z, y, low, up, x_at, residual, scalars, slots, x_out, z_out, y_out, pushed):
    join(pushed, mine, other)
    rho, alpha = scalars[0:1, :], scalars[2:3, :]
    step = step_of(mine, other, rho[:, 0:1])
    z_next, y_next = update(pushed[...], image[...], z[...], y[...], low[...], up[...], step, rho, alpha)
    z_out[...] = z_next
    y_out[...] = y_next
    x = x_at[...] + (alpha * step) * residual[...]
    size = x_at.shape[1]
    part = size // slots
    if slots > 1:
        x = pltpu.roll(x, lax.rem(slots - lax.axis_index("row"), slots) * part, 1)
    x_out[...] = x[:, :part]


def flip(size, step):
    return [(i, i ^ step) for i in range(size)]


def butterfly(value, axis, size, first=1):
    step = first
    while step < size:
        value = value + lax.ppermute(value, axis, flip(size, step))
        step *= 2
    return value


def shards(n_row, n_col, tile_values, tile_rows, tile_cols, x, z, y, low, up, d, q, penalty, proximal, relaxation):
    count, size = tile_values.shape[2], tile_values.shape[3]
    tiles = tile_values.reshape(count, size, size)
    rows, cols = tile_rows.reshape(1, count), tile_cols.reshape(1, count)
    bz, (bx, part) = z.shape[0], x.shape
    half = bz // 2
    big = pltpu.VMEM((bz, size), F32)
    small = pltpu.VMEM((bx, size), F32)
    out_big = jax.ShapeDtypeStruct((bz, size), F32)

    def call(kernel, name, out_shape, scratch=()):
        def run(*args):
            args = [pltpu.with_memory_space_constraint(a, pltpu.VMEM) for a in args]
            return pl.pallas_call(
                kernel,
                out_shape=out_shape,
                in_specs=[VMEM] * len(args),
                out_specs=[VMEM] * len(out_shape),
                scratch_shapes=list(scratch),
                compiler_params=pltpu.CompilerParams(vmem_limit_bytes=LIMIT),
                name=name,
            )(*args)

        return run

    pieces = [lax.ppermute(x, "row", [(i, (i + s) % n_row) for i in range(n_row)]) for s in range(1, n_row)]

    chunks = 8 if count % 8 == 0 else 1
    given = [pltpu.with_memory_space_constraint(a, pltpu.HBM) for a in (tiles, rows, cols, x, d, q)]
    packed, turned, row_table, col_table, row_pick, col_pick, x_at, d_at, q_at = pl.pallas_call(
        functools.partial(prepare_kernel, bz, bx),
        in_specs=[pl.BlockSpec(memory_space=pltpu.HBM)] * 6,
        out_specs=[VMEM] * 9,
        out_shape=[
            pltpu.VMEM((count, size, 2 * size), BF16),
            pltpu.VMEM((count, size, 2 * size), BF16),
            pltpu.VMEM((bz, 3 * count), BF16),
            pltpu.VMEM((bx, 3 * count), BF16),
            pltpu.VMEM((count, bz), BF16),
            pltpu.VMEM((count, bx), BF16),
            small,
            small,
            small,
        ],
        scratch_shapes=[pltpu.VMEM((count, size, size), F32)]
        + [pltpu.VMEM((1, count), jnp.int32)] * 2
        + [pltpu.VMEM((bx, part), F32)] * 3
        + [pltpu.SemaphoreType.DMA((chunks + 5,))],
        compiler_params=pltpu.CompilerParams(vmem_limit_bytes=LIMIT),
        name="prepare",
    )(*given)
    scalars = jnp.stack([penalty[0], proximal[0], relaxation[0]])
    scalars = jnp.broadcast_to(jnp.pad(scalars, (0, SUB - 3))[:, None], (SUB, size))

    bits = [1 << i for i in range(1, n_col.bit_length() - 1)]

    def by_bits(value, some):
        some = list(some)
        if len(some) % 2:
            value = value + lax.ppermute(value, "col", flip(n_col, some.pop(0)))
        while some:
            one, two = some[0], some[1]
            both = lax.ppermute(value, "col", flip(n_col, one | two))
            first = lax.ppermute(value, "col", flip(n_col, one))
            second = lax.ppermute(value, "col", flip(n_col, two))
            value = (value + first) + (second + both)
            some = some[2:]
        return value

    def core_sum(mine, other):
        return mine + lax.ppermute(other, "col", flip(n_col, 1))

    def reduce_half(mine, other):
        return by_bits(core_sum(mine, other), bits)

    def reduce_pushed(mine, other):
        value = core_sum(mine, other)
        if n_row == 2 and bits:
            value = by_bits(value, bits[1:])
            across = lambda mask: lax.ppermute(value, ("row", "col"), flip(n_row * n_col, mask))
            far = across(n_col | bits[0])
            here, beside = across(bits[0]), across(n_col)
            value = value + here
            away = beside + far
            squares = jnp.sum(value[:half] ** 2, axis=0, keepdims=True) + jnp.sum(away[:half] ** 2, axis=0, keepdims=True)
            bent = value[half + 1 : half + 2] + away[half + 1 : half + 2]
        else:
            value = by_bits(value, bits)
            squares = jnp.sum(value[:half] ** 2, axis=0, keepdims=True)
            sums = butterfly(jnp.concatenate([squares, value[half + 1 :]], axis=0), "row", n_row)
            squares, bent = sums[0:1], sums[1:2]
        below = [value[half : half + 1], squares, bent, value[half + 3 :]]
        mine = jnp.concatenate([value[:half]] + below, axis=0)
        return mine, swap(mine)

    def swap(mine):
        return lax.ppermute(mine, "col", flip(n_col, 1))

    halves = [pltpu.VMEM((half, size), F32)] * 2
    mine, other = call(functools.partial(first_kernel, n_row - 1), "first", halves)(
        x_at, *pieces, turned, col_pick, row_table
    )
    mine = reduce_half(mine, other)
    partial, image = call(back_kernel, "back", [small, big])(
        mine, swap(mine), z, y, x_at, d_at, q_at, scalars, packed, row_pick, col_table
    )
    tall = [pltpu.VMEM((half + SUB, size), F32)] * 2
    for turn in range(ADMM_ITERS):
        own = butterfly(partial, "row", n_row // 2) if n_row > 1 else partial
        received = lax.ppermute(own, "row", flip(n_row, n_row // 2)) if n_row > 1 else jnp.zeros_like(own)

        def forward_body(a, b, c, e, *rest):
            forward_kernel(a, b, c, e, n_row, *rest)

        mine, other, residual = call(forward_body, "forward", tall + [small])(
            own, received, d_at, scalars, turned, col_pick, row_table
        )
        mine, other = reduce_pushed(mine, other)
        if turn + 1 < ADMM_ITERS:

            def middle_body(*refs):
                middle_kernel(*refs[:12], n_row, *refs[12:])

            partial, image, z, y, x_at = call(middle_body, "middle", [small, big, big, big, small])(
                mine, other, image, z, y, low, up, x_at, residual, d_at, q_at, scalars, packed, row_pick, col_table
            )
        else:

            def last_body(*refs):
                last_kernel(*refs[:10], n_row, *refs[10:])

            shapes = [jax.ShapeDtypeStruct((bx, part), F32), out_big, out_big]
            return tuple(
                call(last_body, "last", shapes, [pltpu.VMEM((bz, size), F32)])(
                    mine, other, image, z, y, low, up, x_at, residual, scalars
                )
            )


def solution(mesh):
    placed = (
        P("row", "col", None, None, None),
        P("row", "col", None),
        P("row", "col", None),
        P("col", "row"),
        P("row", None),
        P("row", None),
        P("row", None),
        P("row", None),
        P("col", "row"),
        P("col", "row"),
        P(),
        P(),
        P(),
    )
    n_row, n_col = mesh.shape["row"], mesh.shape["col"]
    return jax.shard_map(
        lambda *args: shards(n_row, n_col, *args),
        mesh=mesh,
        in_specs=placed,
        out_specs=(P("col", "row"), P("row", None), P("row", None)),
        check_vma=False,
    )
```

```python
import functools

import jax
import jax.numpy as jnp
from jax import lax
from jax.experimental import pallas as pl
from jax.experimental.pallas import tpu as pltpu
from jax.sharding import PartitionSpec as P

ADMM_ITERS = 2
SUB = 8
F32 = jnp.float32
BF16 = jnp.bfloat16
LIMIT = 24 << 20


VMEM = pl.BlockSpec(memory_space=pltpu.VMEM)


def split2(value):
    high = value.astype(BF16).astype(F32)
    return high, (value - high).astype(BF16).astype(F32)


def split3(value):
    high = value.astype(BF16)
    rest = value - high.astype(F32)
    mid = rest.astype(BF16)
    return high, mid, (rest - mid.astype(F32)).astype(BF16)


def place(piece, slot, width):
    blocks, part = piece.shape
    if part == width:
        return piece
    full = jnp.concatenate([piece, jnp.zeros((blocks, width - part), F32)], axis=1)
    return pltpu.roll(full, slot * part, 1)


def lane_total(row):
    return jnp.sum(row, axis=1, keepdims=True)


def pick(table, value):
    parts = jnp.concatenate(split2(value), axis=1).astype(BF16)
    return lax.dot_general(table[...], parts, (((1,), (0,)), ((), ())), preferred_element_type=F32)


def scatter(table, prod):
    parts = jnp.concatenate(split3(prod), axis=0)
    return lax.dot_general(table[...], parts, (((1,), (0,)), ((), ())), preferred_element_type=F32)


def product(picked, upper, lower):
    count, size = upper.shape[0], upper.shape[1]
    row = lax.broadcasted_iota(jnp.int32, (SUB, size), 0)
    blocks = []
    for m in range(0, count, SUB):
        left = jnp.concatenate([picked[m : m + SUB, :size], picked[m : m + SUB, size:]], axis=0).astype(BF16)
        block = jnp.zeros((SUB, size), F32)
        for k in range(SUB):
            tile = jnp.concatenate([upper[m + k], lower[m + k]], axis=1)
            out = lax.dot_general(left, tile, (((1,), (0,)), ((), ())), preferred_element_type=F32)
            out = out[:SUB] + out[SUB:]
            block = jnp.where(row == k, out[:, :size] + out[:, size:], block)
        blocks.append(block)
    return jnp.concatenate(blocks, axis=0)


def upright(row):
    count = row.shape[1]
    shape = (count, count)
    here = lax.broadcasted_iota(jnp.int32, shape, 0) == lax.broadcasted_iota(jnp.int32, shape, 1)
    return jnp.sum(jnp.where(here, row.astype(F32), 0.0), axis=1, keepdims=True)


def named(column, blocks):
    lane = lax.broadcasted_iota(jnp.int32, (column.shape[0], blocks), 1).astype(F32)
    return jnp.where(lane == column, 1.0, 0.0).astype(BF16)


def prepare_kernel(blocks_z, blocks_x, tiles, rows, cols, x, d, q, upper, lower, row_table, col_pick, x_at, d_at, q_at, held, rows_v, cols_v, x_v, d_v, q_v, sems):
    size = tiles.shape[2]
    count = tiles.shape[0]
    small = [(rows, rows_v), (cols, cols_v), (x, x_v), (d, d_v), (q, q_v)]
    chunks = sems.shape[0] - len(small)
    cuts = [count * i // chunks for i in range(chunks + 1)]
    fetches = [pltpu.make_async_copy(ref, out, sems.at[chunks + i]) for i, (ref, out) in enumerate(small)]
    copies = [
        pltpu.make_async_copy(tiles.at[cuts[i] : cuts[i + 1]], held.at[cuts[i] : cuts[i + 1]], sems.at[i])
        for i in range(chunks)
    ]
    for copy in fetches + copies:
        copy.start()
    for copy in fetches:
        copy.wait()
    half = blocks_z // 2
    core = lax.rem(lax.axis_index("col"), 2)
    spot = lax.broadcasted_iota(jnp.int32, (blocks_z, count), 0) + core * half
    spot = jnp.where(spot >= blocks_z, spot - blocks_z, spot)
    hit = jnp.where(spot == rows_v[...], 1.0, 0.0)
    row_table[...] = jnp.concatenate([hit, hit, hit], axis=1).astype(BF16)
    col_pick[...] = named(upright(cols_v[...]), blocks_x)
    slot = lax.axis_index("row")
    for ref, out in ((x_v, x_at), (d_v, d_at), (q_v, q_at)):
        out[...] = place(ref[...], slot, size)
    for i, copy in enumerate(copies):
        copy.wait()
        for k in range(cuts[i], cuts[i + 1]):
            value = held[k]
            high = value.astype(BF16)
            low = (value - high.astype(F32)).astype(BF16)
            upper[k] = high.T
            lower[k] = low.T


def finish_kernel(upper, lower, rows, cols, upper_out, lower_out, col_table, row_pick):
    count = upper.shape[0]
    blocks_x, blocks_z = col_table.shape[0], row_pick.shape[1]
    hit = jnp.where(lax.broadcasted_iota(jnp.int32, (blocks_x, count), 0) == cols[...], 1.0, 0.0)
    col_table[...] = jnp.concatenate([hit, hit, hit], axis=1).astype(BF16)
    row_pick[...] = named(upright(rows[...]), blocks_z)
    for k in range(count):
        upper_out[k] = upper[k].T
        lower_out[k] = lower[k].T


def first_kernel(others, x_at, *refs):
    pieces, (upper, lower, pick_table, row_table, mine, other) = refs[:others], refs[others:]
    size = x_at.shape[1]
    n_row = others + 1
    full = x_at[...]
    for k in range(others):
        full = full + place(pieces[k][...], lax.rem(lax.axis_index("row") + n_row - 1 - k, n_row), size)
    out = scatter(row_table, product(pick(pick_table, full), upper, lower))
    half = mine.shape[0]
    mine[...] = out[:half]
    other[...] = out[half:]


def forward_kernel(own, received, d_at, sigma, slots, upper, lower, pick_table, row_table, mine, other, residual):
    r = own[...] + received[...]
    residual[...] = r
    out = scatter(row_table, product(pick(pick_table, r), upper, lower))
    half = out.shape[0] // 2
    mine[:half] = out[:half]
    other[:half] = out[half:]
    size = r.shape[1]
    part = size // slots
    lane = lax.broadcasted_iota(jnp.int32, (1, size), 1)
    slot = lax.axis_index("row")
    here = jnp.where((lane >= slot * part) & (lane < (slot + 1) * part), 1.0, 0.0)
    bent = (d_at[...] + sigma[...] * here) * r * r
    extra = jnp.concatenate(
        [jnp.sum(r * r, axis=0, keepdims=True), jnp.sum(bent, axis=0, keepdims=True), jnp.zeros((SUB - 2, size), F32)],
        axis=0,
    )
    mine[half:] = extra
    other[half:] = extra


def join(target, mine, other):
    half = target.shape[0] // 2
    core = lax.rem(lax.axis_index("col"), 2)
    target[pl.ds(pl.multiple_of(core * half, SUB), half), :] = mine[:half]
    target[pl.ds(pl.multiple_of((1 - core) * half, SUB), half), :] = other[:half]


def back_kernel(mine, other, z, y, x_at, d_at, q_at, rho, upper, lower, pick_table, col_table, partial, image):
    join(image, mine, other)
    target = rho[...] * (z[...] - image[...]) - y[...]
    out = scatter(col_table, product(pick(pick_table, target), upper, lower))
    partial[...] = out - q_at[...] - d_at[...] * x_at[...]


def step_of(mine, other, rho):
    half = mine.shape[0] - SUB
    spread = mine[half + 1 : half + 2] + other[half + 1 : half + 2]
    return lane_total(mine[half : half + 1]) / (lane_total(mine[half + 2 : half + 3]) + rho * lane_total(spread))


def update(pushed, image, z, y, low, up, step, rho, alpha):
    mixed = alpha * (image + step * pushed) + (1.0 - alpha) * z
    z_new = jnp.minimum(jnp.maximum(mixed + y / rho, low), up)
    return z_new, y + rho * (mixed - z_new)


def middle_kernel(mine, other, image, z, y, low, up, x_at, residual, d_at, q_at, penalty, relaxation, slots, upper, lower, pick_table, col_table, partial, image_new, z_new, y_new, x_new):
    join(image_new, mine, other)
    rho, alpha = penalty[...], relaxation[...]
    step = step_of(mine, other, rho[:, 0:1])
    pushed = image_new[...]
    z_next, y_next = update(pushed, image[...], z[...], y[...], low[...], up[...], step, rho, alpha)
    fresh = image[...] + (alpha * step) * pushed
    image_new[...] = fresh
    z_new[...] = z_next
    y_new[...] = y_next
    out = scatter(col_table, product(pick(pick_table, rho * z_next - y_next - rho * fresh), upper, lower))
    size = x_at.shape[1]
    part = size // slots
    lane = lax.broadcasted_iota(jnp.int32, (1, size), 1)
    slot = lax.axis_index("row")
    here = jnp.where((lane >= slot * part) & (lane < (slot + 1) * part), 1.0, 0.0)
    x = x_at[...] + (alpha * step * here) * residual[...]
    x_new[...] = x
    partial[...] = out - q_at[...] - d_at[...] * x


def last_kernel(mine, other, image, z, y, low, up, x_at, residual, penalty, relaxation, slots, x_out, z_out, y_out, pushed):
    join(pushed, mine, other)
    rho, alpha = penalty[...], relaxation[...]
    step = step_of(mine, other, rho[:, 0:1])
    z_next, y_next = update(pushed[...], image[...], z[...], y[...], low[...], up[...], step, rho, alpha)
    z_out[...] = z_next
    y_out[...] = y_next
    x = x_at[...] + (alpha * step) * residual[...]
    size = x_at.shape[1]
    part = size // slots
    if slots > 1:
        x = pltpu.roll(x, lax.rem(slots - lax.axis_index("row"), slots) * part, 1)
    x_out[...] = x[:, :part]


def flip(size, step):
    return [(i, i ^ step) for i in range(size)]


def butterfly(value, axis, size, first=1):
    step = first
    while step < size:
        value = value + lax.ppermute(value, axis, flip(size, step))
        step *= 2
    return value


def shards(n_row, n_col, tile_values, tile_rows, tile_cols, x, z, y, low, up, d, q, penalty, proximal, relaxation):
    count, size = tile_values.shape[2], tile_values.shape[3]
    tiles = tile_values.reshape(count, size, size)
    rows, cols = tile_rows.reshape(1, count), tile_cols.reshape(1, count)
    bz, (bx, part) = z.shape[0], x.shape
    half = bz // 2
    big = pltpu.VMEM((bz, size), F32)
    small = pltpu.VMEM((bx, size), F32)
    out_big = jax.ShapeDtypeStruct((bz, size), F32)

    def call(kernel, name, out_shape, scratch=()):
        def run(*args):
            args = [pltpu.with_memory_space_constraint(a, pltpu.VMEM) for a in args]
            return pl.pallas_call(
                kernel,
                out_shape=out_shape,
                in_specs=[VMEM] * len(args),
                out_specs=[VMEM] * len(out_shape),
                scratch_shapes=list(scratch),
                compiler_params=pltpu.CompilerParams(vmem_limit_bytes=LIMIT),
                name=name,
            )(*args)

        return run

    pieces = [lax.ppermute(x, "row", [(i, (i + s) % n_row) for i in range(n_row)]) for s in range(1, n_row)]

    chunks = min(4, count)
    given = [pltpu.with_memory_space_constraint(a, pltpu.HBM) for a in (tiles, rows, cols, x, d, q)]
    *turned, row_table, col_pick, x_at, d_at, q_at = pl.pallas_call(
        functools.partial(prepare_kernel, bz, bx),
        in_specs=[pl.BlockSpec(memory_space=pltpu.HBM)] * 6,
        out_specs=[VMEM] * 7,
        out_shape=[
            pltpu.VMEM((count, size, size), BF16),
            pltpu.VMEM((count, size, size), BF16),
            pltpu.VMEM((bz, 3 * count), BF16),
            pltpu.VMEM((count, bx), BF16),
            small,
            small,
            small,
        ],
        scratch_shapes=[pltpu.VMEM((count, size, size), F32)]
        + [pltpu.VMEM((1, count), jnp.int32)] * 2
        + [pltpu.VMEM((bx, part), F32)] * 3
        + [pltpu.SemaphoreType.DMA((chunks + 5,))],
        compiler_params=pltpu.CompilerParams(vmem_limit_bytes=LIMIT),
        name="prepare",
    )(*given)
    rho, sigma, alpha = (jnp.broadcast_to(a, (1, size)) for a in (penalty, proximal, relaxation))
    bits = [1 << i for i in range(1, n_col.bit_length() - 1)]

    def by_bits(value, some):
        some = list(some)
        if len(some) % 2:
            value = value + lax.ppermute(value, "col", flip(n_col, some.pop(0)))
        while some:
            one, two = some[0], some[1]
            both = lax.ppermute(value, "col", flip(n_col, one | two))
            first = lax.ppermute(value, "col", flip(n_col, one))
            second = lax.ppermute(value, "col", flip(n_col, two))
            value = (value + first) + (second + both)
            some = some[2:]
        return value

    def core_sum(mine, other):
        return mine + lax.ppermute(other, "col", flip(n_col, 1))

    def reduce_half(mine, other):
        if not bits:
            return core_sum(mine, other)
        beside = lax.ppermute(mine, "col", flip(n_col, bits[0]))
        across = lax.ppermute(other, "col", flip(n_col, 1 | bits[0]))
        near = lax.ppermute(other, "col", flip(n_col, 1))
        return by_bits((mine + near) + (beside + across), bits[1:])

    def reduce_pushed(mine, other):
        value = core_sum(mine, other)
        if n_row == 2 and bits:
            value = by_bits(value, bits[1:])
            across = lambda mask: lax.ppermute(value, ("row", "col"), flip(n_row * n_col, mask))
            far = across(n_col | bits[0])
            here, beside = across(bits[0]), across(n_col)
            value = value + here
            away = beside + far
            squares = jnp.sum(value[:half] ** 2, axis=0, keepdims=True) + jnp.sum(away[:half] ** 2, axis=0, keepdims=True)
            bent = value[half + 1 : half + 2] + away[half + 1 : half + 2]
        else:
            value = by_bits(value, bits)
            squares = jnp.sum(value[:half] ** 2, axis=0, keepdims=True)
            sums = butterfly(jnp.concatenate([squares, value[half + 1 :]], axis=0), "row", n_row)
            squares, bent = sums[0:1], sums[1:2]
        below = [value[half : half + 1], squares, bent, value[half + 3 :]]
        mine = jnp.concatenate([value[:half]] + below, axis=0)
        return mine, swap(mine)

    def swap(mine):
        return lax.ppermute(mine, "col", flip(n_col, 1))

    halves = [pltpu.VMEM((half, size), F32)] * 2
    mine, other = call(functools.partial(first_kernel, n_row - 1), "first", halves)(
        x_at, *pieces, *turned, col_pick, row_table
    )
    mine = reduce_half(mine, other)
    tables = [
        pltpu.VMEM((count, size, size), BF16),
        pltpu.VMEM((count, size, size), BF16),
        pltpu.VMEM((bx, 3 * count), BF16),
        pltpu.VMEM((count, bz), BF16),
    ]
    *packed, col_table, row_pick = call(finish_kernel, "finish", tables)(*turned, rows, cols)
    mine, packed, col_table, row_pick = lax.optimization_barrier((mine, packed, col_table, row_pick))
    partial, image = call(back_kernel, "back", [small, big])(
        mine, swap(mine), z, y, x_at, d_at, q_at, rho, *packed, row_pick, col_table
    )
    tall = [pltpu.VMEM((half + SUB, size), F32)] * 2
    for turn in range(ADMM_ITERS):
        own = butterfly(partial, "row", n_row // 2) if n_row > 1 else partial
        received = lax.ppermute(own, "row", flip(n_row, n_row // 2)) if n_row > 1 else jnp.zeros_like(own)

        def forward_body(a, b, c, e, *rest):
            forward_kernel(a, b, c, e, n_row, *rest)

        mine, other, residual = call(forward_body, "forward", tall + [small])(
            own, received, d_at, sigma, *turned, col_pick, row_table
        )
        mine, other = reduce_pushed(mine, other)
        if turn + 1 < ADMM_ITERS:

            def middle_body(*refs):
                middle_kernel(*refs[:13], n_row, *refs[13:])

            partial, image, z, y, x_at = call(middle_body, "middle", [small, big, big, big, small])(
                mine, other, image, z, y, low, up, x_at, residual, d_at, q_at, rho, alpha, *packed, row_pick, col_table
            )
        else:

            def last_body(*refs):
                last_kernel(*refs[:11], n_row, *refs[11:])

            shapes = [jax.ShapeDtypeStruct((bx, part), F32), out_big, out_big]
            return tuple(
                call(last_body, "last", shapes, [pltpu.VMEM((bz, size), F32)])(
                    mine, other, image, z, y, low, up, x_at, residual, rho, alpha
                )
            )


def solution(mesh):
    placed = (
        P("row", "col", None, None, None),
        P("row", "col", None),
        P("row", "col", None),
        P("col", "row"),
        P("row", None),
        P("row", None),
        P("row", None),
        P("row", None),
        P("col", "row"),
        P("col", "row"),
        P(),
        P(),
        P(),
    )
    n_row, n_col = mesh.shape["row"], mesh.shape["col"]
    return jax.shard_map(
        lambda *args: shards(n_row, n_col, *args),
        mesh=mesh,
        in_specs=placed,
        out_specs=(P("col", "row"), P("row", None), P("row", None)),
        check_vma=False,
    )
```
